1024 devices in a mesh: grid: 32 (over y_lo, z, core), band: 32 (over y_hi, x).
Axes of the slice: x: 8, y: 8 (y_hi: 4, y_lo: 2; y = y_hi * 2 + y_lo), z: 8, core: 2. Of those that a mesh axis runs over, the one named last changes fastest.
Arguments:
- orbitals: bfloat16 [32768, 4096], P('grid', 'band'), may hold values from -6 to 6
- points: int32 [4096], replicated, may hold values from 0 to 32767, as said below
- theta: bfloat16 [32768, 4096], P('grid'), may hold values from -0.09375 to 0.09375
- metric: float32 [4096, 4096], P('grid', 'band'), may hold values from -0.09375 to 0.09375
Outputs:
- applied: bfloat16 [32768, 4096], P('grid', 'band')
The draws below stay inside these ranges and needn't reach their ends.
Inputs may be any that keep to these rules, and one draw needn't show every extreme that they name: The 4096 points are distinct grid indices in random order; every block of 1024 consecutive grid indices holds the same number of them.
All inputs are finite; a program needn't handle non-finite values.
Results may differ from the reference program's by a relative error of at most 0.0057.
Values may be sent and summed in bfloat16 or wider, within the bound.
No kernel may reach another device: no remote copies, remote signals or barrier semaphores. Data moves between devices by JAX's collectives and lax.ppermute only.
A program may use at most 64 MiB of HBM per device.

```python
import jax
import jax.numpy as jnp
from jax import lax

NMU = 4096
NB = 4096
ROWS_DEV = 1024
NG = 32768


def draw_points(key, part):
    devices = NG // ROWS_DEV
    per_device = NMU // devices
    keys = jax.random.split(key, devices)
    shuffled = jax.vmap(lambda single: jax.random.permutation(single, ROWS_DEV - 2))(keys).astype(jnp.int32) + 1
    chosen = shuffled[:, :per_device]
    device_ids = jnp.arange(devices, dtype=jnp.int32)
    first_col = jnp.where(device_ids == 0, 0, jnp.where(device_ids == devices - 1, ROWS_DEV - 1, chosen[:, 0]))
    chosen = chosen.at[:, 0].set(first_col.astype(jnp.int32))
    global_ids = (chosen + device_ids[:, None] * ROWS_DEV).reshape(-1)
    order = jax.random.permutation(jax.random.fold_in(key, 7), NMU)
    return global_ids[order].astype(jnp.int32)


def level_of(own_key, extent, cuts, least, high):
    level = 1.0
    for dim, blocks in cuts:
        heights = jax.random.uniform(jax.random.fold_in(jax.random.fold_in(own_key, 6), dim), (blocks,), jnp.float32, least / len(cuts), high / len(cuts))
        level = level * jnp.repeat(jnp.exp(heights), extent[dim] // blocks).reshape((-1,) + (1,) * (len(extent) - 1 - dim))
    return level


def scatter_about(own_key, dims, scale, reach, pieces=(), kind=jnp.bfloat16):
    entries = jax.random.normal(own_key, dims, jnp.float32) * scale
    if len(pieces) > 0:
        entries = level_of(own_key, dims, pieces, -0.22, 0.18) * entries
    return jnp.clip(entries, min=-reach, max=reach).astype(kind)


def setup_inputs(seed: int = 0) -> dict:
    arg_keys = jax.random.split(jax.random.key(seed), 5)
    return {
        "orbitals": scatter_about(arg_keys[0], (NG, NB), 1.0, 6.0, ((0, 32), (1, 32))),
        "points": draw_points(jax.random.fold_in(arg_keys[4], 71), 0),
        "theta": scatter_about(arg_keys[2], (NG, NMU), NMU ** -0.5, 0.09375, ((0, 32),)),
        "metric": scatter_about(arg_keys[3], (NMU, NMU), NMU ** -0.5, 0.09375, ((0, 32), (1, 32)), jnp.float32),
    }


def reference(orbitals, points, theta, metric):
    sampled = jnp.take(orbitals, points.astype(jnp.int32), axis=0)
    wide = sampled.astype(jnp.float32)
    density = jnp.dot(wide, wide.T, precision=lax.Precision.HIGHEST) * (1.0 / NB)
    squared = density * density
    kernel = jnp.dot(squared, metric, precision=lax.Precision.HIGHEST).astype(jnp.bfloat16)
    coeffs = jnp.dot(kernel.astype(jnp.float32), wide, precision=lax.Precision.HIGHEST).astype(jnp.bfloat16)
    applied = jnp.dot(theta.astype(jnp.float32), coeffs.astype(jnp.float32), precision=lax.Precision.HIGHEST)
    return applied.astype(jnp.bfloat16)
```

```python
import jax
import jax.numpy as jnp
from jax import lax
from jax.sharding import PartitionSpec as P

NB = 4096
Y, Z, CORE = 2, 8, 2


def grid_index(y, z, core):
    return (y * Z + z) * CORE + core


Z_GROUPS = [[grid_index(y, z, c) for z in range(Z)] for y in range(Y) for c in range(CORE)]
YC_GROUPS = [[grid_index(y, z, c) for y in range(Y) for c in range(CORE)] for z in range(Z)]


def spread(x, count):
    return jnp.broadcast_to(x[None], (count, *x.shape))


def gather_grid(x):
    along_z = lax.all_to_all(spread(x, Z), "grid", 0, 0, axis_index_groups=Z_GROUPS, tiled=True)
    groups = lax.all_to_all(spread(along_z, Y * CORE), "grid", 0, 0, axis_index_groups=YC_GROUPS, tiled=True)
    return groups.reshape(Y * CORE * Z, *x.shape)


def exchange_band(blocks):
    return lax.all_to_all(blocks, "band", 0, 0, tiled=True)


def in_gather_order(block):
    return (block // (Z * CORE) * CORE + block % CORE) * Z + block // CORE % Z


def blocks_in_gather_order(blocks):
    shape = blocks.shape
    return blocks.reshape(Y, Z, CORE, *shape[1:]).swapaxes(1, 2).reshape(shape)


def shards(orbitals, points, theta, metric):
    row_count = orbitals.shape[0]
    point_count = points.shape[0]
    grid_count, band_count = lax.axis_size("grid"), lax.axis_size("band")
    me = lax.axis_index("grid")
    own = point_count // grid_count
    slots = jnp.arange(point_count, dtype=jnp.int32)
    by_owner, order = lax.sort_key_val(points, slots)
    my_rows = lax.dynamic_slice_in_dim(by_owner, me * own, own, 0) - me * row_count
    packed = jnp.take(orbitals, my_rows, axis=0, mode="clip")
    gathered = gather_grid(packed).reshape(point_count, -1)
    placing = lax.sort_key_val(order, slots)[1]
    placing = in_gather_order(placing // own) * own + placing % own
    sampled = jnp.take(gathered, placing, axis=0, mode="clip")
    sampled = sampled.reshape(grid_count, own, -1)

    mine = in_gather_order(me)
    my_points = lax.dynamic_index_in_dim(sampled, mine, 0, keepdims=False)
    partial_rows = lax.dot_general(
        blocks_in_gather_order(sampled), my_points, (((2,), (1,)), ((), ())), preferred_element_type=jnp.float32
    )
    density = jnp.sum(exchange_band(partial_rows), axis=0) * (1.0 / NB)
    squared = exchange_band(spread(density * density, band_count))

    metric_rows = exchange_band(spread(metric, band_count))
    product = lax.dot_general(
        metric_rows,
        sampled.astype(jnp.float32),
        (((0, 2), (0, 1)), ((), ())),
        precision=lax.Precision.HIGH,
        preferred_element_type=jnp.float32,
    )
    coeffs = lax.dot_general(
        squared,
        gather_grid(product),
        (((0, 1), (0, 1)), ((), ())),
        precision=lax.Precision.HIGH,
        preferred_element_type=jnp.float32,
    ).astype(jnp.bfloat16)
    coeffs = gather_grid(coeffs).reshape(point_count, -1)
    return jnp.dot(theta, coeffs, preferred_element_type=jnp.float32).astype(jnp.bfloat16)


def solution(mesh):
    placed = (P("grid", "band"), P(), P("grid", None), P("grid", "band"))
    return jax.shard_map(
        shards, mesh=mesh, in_specs=placed, out_specs=P("grid", "band"), check_vma=False
    )
```

```python
import jax
import jax.numpy as jnp
from jax import lax
from jax.sharding import PartitionSpec as P

NB = 4096
Y, Z, CORE = 2, 8, 2


def grid_index(y, z, core):
    return (y * Z + z) * CORE + core


Z_GROUPS = [[grid_index(y, z, c) for z in range(Z)] for y in range(Y) for c in range(CORE)]
YC_GROUPS = [[grid_index(y, z, c) for y in range(Y) for c in range(CORE)] for z in range(Z)]
GRID_BITS = (8, 4, 2, 16, 1)
BAND_BITS = (16, 8, 4, 2, 1)


def spread(x, count):
    return jnp.broadcast_to(x[None], (count, *x.shape))


def gather_z(x):
    return lax.all_to_all(spread(x, Z), "grid", 0, 0, axis_index_groups=Z_GROUPS, tiled=True)


def gather_yc(along_z):
    groups = lax.all_to_all(spread(along_z, Y * CORE), "grid", 0, 0, axis_index_groups=YC_GROUPS, tiled=True)
    return groups.reshape(Y * CORE * Z, *along_z.shape[1:])


def exchange_band(blocks):
    return lax.all_to_all(blocks, "band", 0, 0, tiled=True)


def gather_doubling(x, axis, bits):
    count = lax.axis_size(axis)
    x = x[None]
    for bit in bits:
        x = jnp.concatenate([x, lax.ppermute(x, axis, [(j, j ^ bit) for j in range(count)])])
    return x


def doubled_place(k, bits):
    return sum((k // bit % 2) << i for i, bit in enumerate(bits))


def in_gather_order(block):
    return (block // (Z * CORE) * CORE + block % CORE) * Z + block // CORE % Z


def take(rows, index):
    return jnp.take(rows, index, axis=0, mode="clip")


def shards(orbitals, points, theta, metric):
    row_count = orbitals.shape[0]
    point_count = points.shape[0]
    grid_count, band_count = lax.axis_size("grid"), lax.axis_size("band")
    me = lax.axis_index("grid")
    own = point_count // grid_count
    slots = jnp.arange(point_count, dtype=jnp.int32)
    by_owner, order = lax.sort_key_val(points, slots)
    my_rows = lax.dynamic_slice_in_dim(by_owner, me * own, own, 0) - me * row_count
    packed = take(orbitals, my_rows)
    along_z = gather_z(packed)
    metric_rows = gather_doubling(metric.astype(jnp.bfloat16), "band", BAND_BITS)
    gathered = gather_yc(along_z).reshape(point_count, -1)
    placing = lax.sort_key_val(order, slots)[1]
    placing = in_gather_order(placing // own) * own + placing % own

    mine = in_gather_order(me)
    my_points = take(gathered, lax.dynamic_slice_in_dim(placing, mine * own, own, 0))
    partial_rows = lax.dot_general(
        gathered, my_points, (((1,), (1,)), ((), ())), preferred_element_type=jnp.float32
    ).astype(jnp.bfloat16)
    partial_rows = exchange_band(partial_rows.reshape(grid_count, own, own))
    blocks = [0] * band_count
    for k in range(band_count):
        blocks[doubled_place(k, BAND_BITS)] = k
    blocks = jnp.asarray(blocks, jnp.int32) ^ lax.axis_index("band")
    sampled = take(gathered, take(placing.reshape(band_count, own), blocks).reshape(point_count))
    product = lax.dot_general(
        metric_rows,
        sampled.reshape(grid_count, own, -1),
        (((0, 2), (0, 1)), ((), ())),
        preferred_element_type=jnp.float32,
    ).astype(jnp.bfloat16)
    products = gather_doubling(product, "grid", GRID_BITS).reshape(point_count, -1)
    density = jnp.sum(partial_rows.astype(jnp.float32), axis=0) * (1.0 / NB)
    squared = (density * density).astype(jnp.bfloat16)
    squared = exchange_band(spread(squared, band_count))
    order = order.reshape(Y, Z, CORE, own).swapaxes(1, 2).reshape(point_count)
    products = take(products, doubled_place(order // own ^ me, GRID_BITS) * own + order % own)
    coeffs = lax.dot_general(
        squared,
        products.reshape(grid_count, own, -1),
        (((0, 1), (0, 1)), ((), ())),
        preferred_element_type=jnp.float32,
    ).astype(jnp.bfloat16)
    coeffs = gather_yc(gather_z(coeffs)).reshape(point_count, -1)
    return jnp.dot(theta, coeffs, preferred_element_type=jnp.float32).astype(jnp.bfloat16)


def solution(mesh):
    placed = (P("grid", "band"), P(), P("grid", None), P("grid", "band"))
    return jax.shard_map(
        shards, mesh=mesh, in_specs=placed, out_specs=P("grid", "band"), check_vma=False
    )
```

```python
import jax
import jax.numpy as jnp
from jax import lax
from jax.experimental import pallas as pl
from jax.experimental.pallas import tpu as pltpu
from jax.sharding import PartitionSpec as P

NB = 4096
Y, Z, CORE = 2, 8, 2


def grid_index(y, z, core):
    return (y * Z + z) * CORE + core


Z_GROUPS = [[grid_index(y, z, c) for z in range(Z)] for y in range(Y) for c in range(CORE)]
YC_GROUPS = [[grid_index(y, z, c) for y in range(Y) for c in range(CORE)] for z in range(Z)]
GRID_BITS = (8, 4, 2, 16, 1)
BAND_BITS = (16, 8, 4, 2, 1)


def spread(x, count):
    return jnp.broadcast_to(x[None], (count, *x.shape))


def gather_z(x):
    return lax.all_to_all(spread(x, Z), "grid", 0, 0, axis_index_groups=Z_GROUPS, tiled=True)


def gather_yc(along_z):
    groups = lax.all_to_all(spread(along_z, Y * CORE), "grid", 0, 0, axis_index_groups=YC_GROUPS, tiled=True)
    return groups.reshape(Y * CORE * Z, *along_z.shape[1:])


def exchange_band(blocks):
    return lax.all_to_all(blocks, "band", 0, 0, tiled=True)


def gather_doubling(x, axis, bits):
    count = lax.axis_size(axis)
    x = x[None]
    for bit in bits:
        x = jnp.concatenate([x, lax.ppermute(x, axis, [(j, j ^ bit) for j in range(count)])])
    return x


def doubled_place(k, bits):
    return sum((k // bit % 2) << i for i, bit in enumerate(bits))


def in_gather_order(block):
    return (block // (Z * CORE) * CORE + block % CORE) * Z + block // CORE % Z


ROWS_A_STEP = 16
ROWS_A_DOT = 256
IN_VMEM = pl.BlockSpec(memory_space=pltpu.VMEM)


def place_kernel(index_ref, rows_ref, placed_ref, wide, placed):
    wide[...] = rows_ref[...].astype(jnp.float32)

    def some(step, carry):
        for i in range(ROWS_A_STEP):
            row = step * ROWS_A_STEP + i
            placed[pl.ds(row, 1), :] = wide[pl.ds(index_ref[row], 1), :]
        return carry

    lax.fori_loop(0, rows_ref.shape[0] // ROWS_A_STEP, some, 0)
    placed_ref[...] = placed[...].astype(placed_ref.dtype)


def place(rows, index):
    return pl.pallas_call(
        place_kernel,
        out_shape=jax.ShapeDtypeStruct(rows.shape, rows.dtype),
        in_specs=[pl.BlockSpec(memory_space=pltpu.SMEM), IN_VMEM],
        out_specs=IN_VMEM,
        scratch_shapes=[pltpu.VMEM(rows.shape, jnp.float32)] * 2,
        compiler_params=pltpu.CompilerParams(vmem_limit_bytes=12 << 20),
        cost_estimate=pl.CostEstimate(flops=0, bytes_accessed=12 * rows.size, transcendentals=0),
        name="place_rows",
    )(index, rows)


def apply_kernel(theta_ref, coeffs_ref, applied_ref):
    applied_ref[...] = jnp.dot(
        theta_ref[...], coeffs_ref[...], preferred_element_type=jnp.float32
    ).astype(applied_ref.dtype)


def apply(theta, coeffs):
    rows, depth, columns = *theta.shape, coeffs.shape[1]
    return pl.pallas_call(
        apply_kernel,
        out_shape=jax.ShapeDtypeStruct((rows, columns), theta.dtype),
        grid=(rows // ROWS_A_DOT,),
        in_specs=[
            pl.BlockSpec((ROWS_A_DOT, depth), lambda i: (i, 0)),
            pl.BlockSpec((depth, columns), lambda i: (0, 0), pipeline_mode=pl.Buffered(1)),
        ],
        out_specs=pl.BlockSpec((ROWS_A_DOT, columns), lambda i: (i, 0)),
        cost_estimate=pl.CostEstimate(
            flops=2 * rows * depth * columns, bytes_accessed=2 * (theta.size + coeffs.size), transcendentals=0
        ),
        name="apply_theta",
    )(theta, coeffs)


def take(rows, index):
    return jnp.take(rows, index, axis=0, mode="clip")


def shards(orbitals, points, theta, metric):
    row_count = orbitals.shape[0]
    point_count = points.shape[0]
    grid_count, band_count = lax.axis_size("grid"), lax.axis_size("band")
    me = lax.axis_index("grid")
    own = point_count // grid_count
    slots = jnp.arange(point_count, dtype=jnp.int32)
    by_owner, order = lax.sort_key_val(points, slots)
    my_rows = lax.dynamic_slice_in_dim(by_owner, me * own, own, 0) - me * row_count
    packed = take(orbitals, my_rows)
    along_z = gather_z(packed)
    metric_rows = gather_doubling(metric.astype(jnp.bfloat16), "band", BAND_BITS)
    gathered = gather_yc(along_z).reshape(point_count, -1)
    placing = lax.sort_key_val(order, slots)[1]
    placing = in_gather_order(placing // own) * own + placing % own

    mine = in_gather_order(me)
    my_points = take(gathered, lax.dynamic_slice_in_dim(placing, mine * own, own, 0))
    partial_rows = lax.dot_general(
        gathered, my_points, (((1,), (1,)), ((), ())), preferred_element_type=jnp.float32
    ).astype(jnp.bfloat16)
    partial_rows = exchange_band(partial_rows.reshape(grid_count, own, own))
    blocks = [0] * band_count
    for k in range(band_count):
        blocks[doubled_place(k, BAND_BITS)] = k
    blocks = jnp.asarray(blocks, jnp.int32) ^ lax.axis_index("band")
    sampled = place(gathered, take(placing.reshape(band_count, own), blocks).reshape(point_count))
    product = lax.dot_general(
        metric_rows,
        sampled.reshape(grid_count, own, -1),
        (((0, 2), (0, 1)), ((), ())),
        preferred_element_type=jnp.float32,
    ).astype(jnp.bfloat16)
    products = gather_doubling(product, "grid", GRID_BITS).reshape(point_count, -1)
    density = jnp.sum(partial_rows.astype(jnp.float32), axis=0) * (1.0 / NB)
    squared = (density * density).astype(jnp.bfloat16)
    squared = exchange_band(spread(squared, band_count))
    order = order.reshape(Y, Z, CORE, own).swapaxes(1, 2).reshape(point_count)
    products = place(products, doubled_place(order // own ^ me, GRID_BITS) * own + order % own)
    coeffs = lax.dot_general(
        squared,
        products.reshape(grid_count, own, -1),
        (((0, 1), (0, 1)), ((), ())),
        preferred_element_type=jnp.float32,
    ).astype(jnp.bfloat16)
    coeffs = gather_yc(gather_z(coeffs)).reshape(point_count, -1)
    return apply(theta, coeffs)


def solution(mesh):
    placed = (P("grid", "band"), P(), P("grid", None), P("grid", "band"))
    return jax.shard_map(
        shards, mesh=mesh, in_specs=placed, out_specs=P("grid", "band"), check_vma=False
    )
```

```python
import jax
import jax.numpy as jnp
from jax import lax
from jax.experimental import pallas as pl
from jax.experimental.pallas import tpu as pltpu
from jax.sharding import PartitionSpec as P

NB = 4096
Y, Z, CORE = 2, 8, 2


def grid_index(y, z, core):
    return (y * Z + z) * CORE + core


Z_GROUPS = [[grid_index(y, z, c) for z in range(Z)] for y in range(Y) for c in range(CORE)]
YC_GROUPS = [[grid_index(y, z, c) for y in range(Y) for c in range(CORE)] for z in range(Z)]
GRID_BITS = (16, 8, 4, 2, 1)
X_BITS, X_FAR, Y_HI = (0, 1, 2, 3), (0, 4), (0, 8, 16, 24)


def spread(x, count):
    return jnp.broadcast_to(x[None], (count, *x.shape))


def gather_z(x):
    return lax.all_to_all(spread(x, Z), "grid", 0, 0, axis_index_groups=Z_GROUPS, tiled=True)


def gather_yc(along_z):
    groups = lax.all_to_all(spread(along_z, Y * CORE), "grid", 0, 0, axis_index_groups=YC_GROUPS, tiled=True)
    return groups.reshape(Y * CORE * Z, *along_z.shape[1:])


def exchange_band(blocks):
    return lax.all_to_all(blocks, "band", 0, 0, tiled=True)


def gather_doubling(x, axis, bits):
    count = lax.axis_size(axis)
    x = x[None]
    for bit in bits:
        x = jnp.concatenate([x, lax.ppermute(x, axis, [(j, j ^ bit) for j in range(count)])])
    return x


def swap(x, axis, bit):
    return lax.ppermute(x, axis, [(i, i ^ bit) for i in range(lax.axis_size(axis))])


def gather_metric(block):
    near = jnp.stack([block, *(swap(block, "band", y) for y in Y_HI[1:])])
    half = jnp.concatenate([near, swap(near, "band", X_FAR[1])])
    return [half, *(swap(half, "band", x) for x in X_BITS[1:])]


def doubled_place(k, bits):
    return sum((k // bit % 2) << i for i, bit in enumerate(bits))


def in_gather_order(block):
    return (block // (Z * CORE) * CORE + block % CORE) * Z + block // CORE % Z


ROWS_A_STEP = 16
ROWS_A_DOT = 256
IN_VMEM = pl.BlockSpec(memory_space=pltpu.VMEM)


def place_kernel(index_ref, rows_ref, placed_ref, wide, placed):
    wide[...] = rows_ref[...].astype(jnp.float32)

    def some(step, carry):
        for i in range(ROWS_A_STEP):
            row = step * ROWS_A_STEP + i
            placed[pl.ds(row, 1), :] = wide[pl.ds(index_ref[row], 1), :]
        return carry

    lax.fori_loop(0, rows_ref.shape[0] // ROWS_A_STEP, some, 0)
    placed_ref[...] = placed[...].astype(placed_ref.dtype)


def place(rows, index):
    return pl.pallas_call(
        place_kernel,
        out_shape=jax.ShapeDtypeStruct(rows.shape, rows.dtype),
        in_specs=[pl.BlockSpec(memory_space=pltpu.SMEM), IN_VMEM],
        out_specs=IN_VMEM,
        scratch_shapes=[pltpu.VMEM(rows.shape, jnp.float32)] * 2,
        compiler_params=pltpu.CompilerParams(vmem_limit_bytes=12 << 20),
        cost_estimate=pl.CostEstimate(flops=0, bytes_accessed=12 * rows.size, transcendentals=0),
        name="place_rows",
    )(index, rows)


def multiply_kernel(*refs):
    *part_refs, rows_ref, product_ref = refs
    blocks, own, _ = part_refs[0].shape
    total = jnp.zeros(product_ref.shape, jnp.float32)
    for i, part_ref in enumerate(part_refs):
        for block in range(blocks):
            rows = rows_ref[pl.ds((i * blocks + block) * own, own), :]
            total += jnp.dot(part_ref[block], rows, preferred_element_type=jnp.float32)
    product_ref[...] = total.astype(product_ref.dtype)


def multiply(parts, rows):
    own, columns = parts[0].shape[1], rows.shape[1]
    return pl.pallas_call(
        multiply_kernel,
        out_shape=jax.ShapeDtypeStruct((own, columns), rows.dtype),
        in_specs=[IN_VMEM] * (len(parts) + 1),
        out_specs=IN_VMEM,
        compiler_params=pltpu.CompilerParams(vmem_limit_bytes=8 << 20),
        cost_estimate=pl.CostEstimate(
            flops=2 * own * rows.size, bytes_accessed=4 * rows.size, transcendentals=0
        ),
        name="multiply_metric",
    )(*parts, rows)


def apply_kernel(theta_ref, coeffs_ref, applied_ref):
    applied_ref[...] = jnp.dot(
        theta_ref[...], coeffs_ref[...], preferred_element_type=jnp.float32
    ).astype(applied_ref.dtype)


def apply(theta, coeffs):
    rows, depth, columns = *theta.shape, coeffs.shape[1]
    return pl.pallas_call(
        apply_kernel,
        out_shape=jax.ShapeDtypeStruct((rows, columns), theta.dtype),
        grid=(rows // ROWS_A_DOT,),
        in_specs=[
            pl.BlockSpec((ROWS_A_DOT, depth), lambda i: (i, 0)),
            pl.BlockSpec((depth, columns), lambda i: (0, 0), pipeline_mode=pl.Buffered(1)),
        ],
        out_specs=pl.BlockSpec((ROWS_A_DOT, columns), lambda i: (i, 0)),
        cost_estimate=pl.CostEstimate(
            flops=2 * rows * depth * columns, bytes_accessed=2 * (theta.size + coeffs.size), transcendentals=0
        ),
        name="apply_theta",
    )(theta, coeffs)


def take(rows, index):
    return jnp.take(rows, index, axis=0, mode="clip")


def shards(orbitals, points, theta, metric):
    row_count = orbitals.shape[0]
    point_count = points.shape[0]
    grid_count, band_count = lax.axis_size("grid"), lax.axis_size("band")
    me = lax.axis_index("grid")
    own = point_count // grid_count
    slots = jnp.arange(point_count, dtype=jnp.int32)
    by_owner, order = lax.sort_key_val(points, slots)
    my_rows = lax.dynamic_slice_in_dim(by_owner, me * own, own, 0) - me * row_count
    packed = take(orbitals, my_rows)
    along_z = gather_z(packed)
    metric_parts = gather_metric(metric.astype(jnp.bfloat16))
    gathered = gather_yc(along_z).reshape(point_count, -1)
    placing = lax.sort_key_val(order, slots)[1]
    placing = in_gather_order(placing // own) * own + placing % own

    mine = in_gather_order(me)
    my_points = take(gathered, lax.dynamic_slice_in_dim(placing, mine * own, own, 0))
    partial_rows = lax.dot_general(
        gathered, my_points, (((1,), (1,)), ((), ())), preferred_element_type=jnp.float32
    ).astype(jnp.bfloat16)
    partial_rows = exchange_band(partial_rows.reshape(grid_count, own, own))
    blocks = [x + far + y for x in X_BITS for far in X_FAR for y in Y_HI]
    blocks = jnp.asarray(blocks, jnp.int32) ^ lax.axis_index("band")
    sampled = place(gathered, take(placing.reshape(band_count, own), blocks).reshape(point_count))
    product = multiply(metric_parts, sampled)
    products = gather_doubling(product, "grid", GRID_BITS).reshape(point_count, -1)
    density = jnp.sum(partial_rows.astype(jnp.float32), axis=0) * (1.0 / NB)
    squared = (density * density).astype(jnp.bfloat16)
    squared = exchange_band(spread(squared, band_count))
    order = order.reshape(Y, Z, CORE, own).swapaxes(1, 2).reshape(point_count)
    products = place(products, doubled_place(order // own ^ me, GRID_BITS) * own + order % own)
    coeffs = lax.dot_general(
        squared,
        products.reshape(grid_count, own, -1),
        (((0, 1), (0, 1)), ((), ())),
        preferred_element_type=jnp.float32,
    ).astype(jnp.bfloat16)
    coeffs = gather_yc(gather_z(coeffs)).reshape(point_count, -1)
    return apply(theta, coeffs)


def solution(mesh):
    placed = (P("grid", "band"), P(), P("grid", None), P("grid", "band"))
    return jax.shard_map(
        shards, mesh=mesh, in_specs=placed, out_specs=P("grid", "band"), check_vma=False
    )
```

```python
import jax
import jax.numpy as jnp
from jax import lax
from jax.experimental import pallas as pl
from jax.experimental.pallas import tpu as pltpu
from jax.sharding import PartitionSpec as P

NB = 4096
Y, Z, CORE = 2, 8, 2


def grid_index(y, z, core):
    return (y * Z + z) * CORE + core


Z_GROUPS = [[grid_index(y, z, c) for z in range(Z)] for y in range(Y) for c in range(CORE)]
YC_GROUPS = [[grid_index(y, z, c) for y in range(Y) for c in range(CORE)] for z in range(Z)]
GRID_BITS = (16, 8, 4, 2, 1)
X_BITS, X_FAR, Y_HI = (0, 1, 2, 3), (0, 4), (0, 8, 16, 24)


def spread(x, count):
    return jnp.broadcast_to(x[None], (count, *x.shape))


def gather_z(x):
    return lax.all_to_all(spread(x, Z), "grid", 0, 0, axis_index_groups=Z_GROUPS, tiled=True)


def gather_yc(along_z):
    groups = lax.all_to_all(spread(along_z, Y * CORE), "grid", 0, 0, axis_index_groups=YC_GROUPS, tiled=True)
    return groups.reshape(Y * CORE * Z, *along_z.shape[1:])


def exchange_band(blocks):
    return lax.all_to_all(blocks, "band", 0, 0, tiled=True)


def gather_doubling(x, axis, bits):
    count = lax.axis_size(axis)
    x = x[None]
    for bit in bits:
        x = jnp.concatenate([x, lax.ppermute(x, axis, [(j, j ^ bit) for j in range(count)])])
    return x


def swap(x, axis, bit):
    return lax.ppermute(x, axis, [(i, i ^ bit) for i in range(lax.axis_size(axis))])


def gather_metric(block):
    near = jnp.stack([block, *(swap(block, "band", y) for y in Y_HI[1:])])
    half = jnp.concatenate([near, swap(near, "band", X_FAR[1])])
    return [half, *(swap(half, "band", x) for x in X_BITS[1:])]


def doubled_place(k, bits):
    return sum((k // bit % 2) << i for i, bit in enumerate(bits))


def in_gather_order(block):
    return (block // (Z * CORE) * CORE + block % CORE) * Z + block // CORE % Z


ROWS_A_STEP = 16
IN_VMEM = pl.BlockSpec(memory_space=pltpu.VMEM)


def place_kernel(index_ref, rows_ref, placed_ref, wide, placed):
    wide[...] = rows_ref[...].astype(jnp.float32)

    def some(step, carry):
        for i in range(ROWS_A_STEP):
            row = step * ROWS_A_STEP + i
            placed[pl.ds(row, 1), :] = wide[pl.ds(index_ref[row], 1), :]
        return carry

    lax.fori_loop(0, rows_ref.shape[0] // ROWS_A_STEP, some, 0)
    placed_ref[...] = placed[...].astype(placed_ref.dtype)


def place(rows, index):
    return pl.pallas_call(
        place_kernel,
        out_shape=jax.ShapeDtypeStruct(rows.shape, rows.dtype),
        in_specs=[pl.BlockSpec(memory_space=pltpu.SMEM), IN_VMEM],
        out_specs=IN_VMEM,
        scratch_shapes=[pltpu.VMEM(rows.shape, jnp.float32)] * 2,
        compiler_params=pltpu.CompilerParams(vmem_limit_bytes=12 << 20),
        cost_estimate=pl.CostEstimate(flops=0, bytes_accessed=12 * rows.size, transcendentals=0),
        name="place_rows",
    )(index, rows)


def multiply_kernel(*refs):
    *part_refs, rows_ref, product_ref = refs
    blocks, own, _ = part_refs[0].shape
    total = jnp.zeros(product_ref.shape, jnp.float32)
    for i, part_ref in enumerate(part_refs):
        for block in range(blocks):
            rows = rows_ref[pl.ds((i * blocks + block) * own, own), :]
            total += jnp.dot(part_ref[block], rows, preferred_element_type=jnp.float32)
    product_ref[...] = total.astype(product_ref.dtype)


def multiply(parts, rows):
    own, columns = parts[0].shape[1], rows.shape[1]
    return pl.pallas_call(
        multiply_kernel,
        out_shape=jax.ShapeDtypeStruct((own, columns), rows.dtype),
        in_specs=[IN_VMEM] * (len(parts) + 1),
        out_specs=IN_VMEM,
        compiler_params=pltpu.CompilerParams(vmem_limit_bytes=8 << 20),
        cost_estimate=pl.CostEstimate(
            flops=2 * own * rows.size, bytes_accessed=4 * rows.size, transcendentals=0
        ),
        name="multiply_metric",
    )(*parts, rows)


BLOCKS_A_STEP = 4


def apply_kernel(_, *refs):
    *theta_refs, part_ref, total_ref, applied_ref, total = refs

    @pl.when(pl.program_id(0) == 0)
    def _():
        total[...] = total_ref[...]

    theta = jnp.concatenate([ref[...] for ref in theta_refs], axis=1)
    part = part_ref[pl.ds(pl.program_id(0) * BLOCKS_A_STEP, BLOCKS_A_STEP)]
    part = part.reshape(theta.shape[1], part_ref.shape[2])
    total[...] += jnp.dot(theta, part, preferred_element_type=jnp.float32)

    @pl.when(pl.program_id(0) == pl.num_programs(0) - 1)
    def _():
        applied_ref[...] = total[...].astype(applied_ref.dtype)


def apply(theta, part, first, total, dtype):
    rows = theta.shape[0]
    blocks, own, columns = part.shape
    if total is None:
        total = jnp.zeros((rows, columns), jnp.float32)

    def theta_spec(k):
        return pl.BlockSpec((rows, own), lambda i, first_ref: (0, first_ref[0] + (i * BLOCKS_A_STEP + k) * CORE))

    return pl.pallas_call(
        apply_kernel,
        out_shape=jax.ShapeDtypeStruct((rows, columns), dtype),
        grid_spec=pltpu.PrefetchScalarGridSpec(
            num_scalar_prefetch=1,
            grid=(blocks // BLOCKS_A_STEP,),
            in_specs=[
                *(theta_spec(k) for k in range(BLOCKS_A_STEP)),
                IN_VMEM,
                IN_VMEM,
            ],
            out_specs=IN_VMEM,
            scratch_shapes=[pltpu.VMEM((rows, columns), jnp.float32)],
        ),
        compiler_params=pltpu.CompilerParams(vmem_limit_bytes=50 << 20),
        cost_estimate=pl.CostEstimate(
            flops=2 * rows * part.size, bytes_accessed=2 * rows * blocks * own, transcendentals=0
        ),
        name="apply_theta",
    )(first.reshape(1), *([theta] * BLOCKS_A_STEP), part, total)


def take(rows, index):
    return jnp.take(rows, index, axis=0, mode="clip")


def shards(orbitals, points, theta, metric):
    row_count = orbitals.shape[0]
    point_count = points.shape[0]
    grid_count, band_count = lax.axis_size("grid"), lax.axis_size("band")
    me = lax.axis_index("grid")
    own = point_count // grid_count
    slots = jnp.arange(point_count, dtype=jnp.int32)
    by_owner, order = lax.sort_key_val(points, slots)
    my_rows = lax.dynamic_slice_in_dim(by_owner, me * own, own, 0) - me * row_count
    packed = take(orbitals, my_rows)
    along_z = gather_z(packed)
    metric_parts = gather_metric(metric.astype(jnp.bfloat16))
    gathered = gather_yc(along_z).reshape(point_count, -1)
    placing = lax.sort_key_val(order, slots)[1]
    placing = in_gather_order(placing // own) * own + placing % own

    my_points = take(gathered, lax.dynamic_slice_in_dim(placing, me * own, own, 0))
    partial_rows = lax.dot_general(
        gathered, my_points, (((1,), (1,)), ((), ())), preferred_element_type=jnp.float32
    ).astype(jnp.bfloat16)
    partial_rows = exchange_band(partial_rows.reshape(grid_count, own, own))
    blocks = [x + far + y for x in X_BITS for far in X_FAR for y in Y_HI]
    blocks = jnp.asarray(blocks, jnp.int32) ^ lax.axis_index("band")
    sampled = place(gathered, take(placing.reshape(band_count, own), blocks).reshape(point_count))
    product = multiply(metric_parts, sampled)
    products = gather_doubling(product, "grid", GRID_BITS).reshape(point_count, -1)
    density = jnp.sum(partial_rows.astype(jnp.float32), axis=0) * (1.0 / NB)
    squared = (density * density).astype(jnp.bfloat16)
    squared = exchange_band(spread(squared, band_count))
    order = order.reshape(Y, Z, CORE, own).swapaxes(1, 2).reshape(point_count)
    products = place(products, doubled_place(order // own ^ me, GRID_BITS) * own + order % own)
    coeffs = lax.dot_general(
        squared,
        products.reshape(grid_count, own, -1),
        (((0, 1), (0, 1)), ((), ())),
        preferred_element_type=jnp.float32,
    ).astype(jnp.bfloat16)
    coeffs = gather_z(coeffs)
    other_y = swap(coeffs, "grid", Z * CORE)
    other_core = swap(coeffs, "grid", 1)
    other_both = swap(other_y, "grid", 1)
    first = me // (Z * CORE) * (Z * CORE) + me % CORE
    total = None
    for name, part, bits in (
        ("own", coeffs, 0),
        ("core", other_core, 1),
        ("y", other_y, Z * CORE),
        ("both", other_both, Z * CORE + 1),
    ):
        dtype = jnp.bfloat16 if name == "both" else jnp.float32
        total = apply(theta, part, first ^ bits, total, dtype)
    return total


def solution(mesh):
    placed = (P("grid", "band"), P(), P("grid", None), P("grid", "band"))
    return jax.shard_map(
        shards, mesh=mesh, in_specs=placed, out_specs=P("grid", "band"), check_vma=False
    )
```

```python
import jax
import jax.numpy as jnp
from jax import lax
from jax.experimental import pallas as pl
from jax.experimental.pallas import tpu as pltpu
from jax.sharding import PartitionSpec as P

NB = 4096
Y, Z, CORE = 2, 8, 2


def grid_index(y, z, core):
    return (y * Z + z) * CORE + core


Z_GROUPS = [[grid_index(y, z, c) for z in range(Z)] for y in range(Y) for c in range(CORE)]
YC_GROUPS = [[grid_index(y, z, c) for y in range(Y) for c in range(CORE)] for z in range(Z)]
GRID_BITS, NEAR_Z = (16, 8, 4, 2, 1), (4, 2, 6)
X_BITS, X_FAR, Y_HI = (0, 1, 2, 3), (0, 4), (0, 8, 16, 24)


def spread(x, count):
    return jnp.broadcast_to(x[None], (count, *x.shape))


def gather_z(x):
    return lax.all_to_all(spread(x, Z), "grid", 0, 0, axis_index_groups=Z_GROUPS, tiled=True)


def gather_yc(along_z):
    groups = lax.all_to_all(spread(along_z, Y * CORE), "grid", 0, 0, axis_index_groups=YC_GROUPS, tiled=True)
    return groups.reshape(Y * CORE * Z, *along_z.shape[1:])


def exchange_band(blocks):
    return lax.all_to_all(blocks, "band", 0, 0, tiled=True)


def gather_doubling(x, axis, bits):
    count = lax.axis_size(axis)
    x = x[None]
    for bit in bits:
        x = jnp.concatenate([x, lax.ppermute(x, axis, [(j, j ^ bit) for j in range(count)])])
    return x


def swap(x, axis, bit):
    return lax.ppermute(x, axis, [(i, i ^ bit) for i in range(lax.axis_size(axis))])


def gather_metric(block):
    near = jnp.stack([block, *(swap(block, "band", y) for y in Y_HI[1:])])
    half = jnp.concatenate([near, swap(near, "band", X_FAR[1])])
    return [half, *(swap(half, "band", x) for x in X_BITS[1:])]


def gather_product(block):
    quarter = gather_doubling(block, "grid", GRID_BITS[:2])
    half = jnp.concatenate([quarter, *(swap(quarter, "grid", z) for z in NEAR_Z)])
    return jnp.concatenate([half, swap(half, "grid", GRID_BITS[4])])


def doubled_place(k, bits):
    return sum((k // bit % 2) << i for i, bit in enumerate(bits))


def in_gather_order(block):
    return (block // (Z * CORE) * CORE + block % CORE) * Z + block // CORE % Z


ROWS_A_STEP = 16
IN_VMEM = pl.BlockSpec(memory_space=pltpu.VMEM)


def place_kernel(index_ref, rows_ref, placed_ref, wide, placed):
    wide[...] = rows_ref[...].astype(jnp.float32)

    def some(step, carry):
        for i in range(ROWS_A_STEP):
            row = step * ROWS_A_STEP + i
            placed[pl.ds(row, 1), :] = wide[pl.ds(index_ref[row], 1), :]
        return carry

    lax.fori_loop(0, rows_ref.shape[0] // ROWS_A_STEP, some, 0)
    placed_ref[...] = placed[...].astype(placed_ref.dtype)


def place(rows, index):
    return pl.pallas_call(
        place_kernel,
        out_shape=jax.ShapeDtypeStruct(rows.shape, rows.dtype),
        in_specs=[pl.BlockSpec(memory_space=pltpu.SMEM), IN_VMEM],
        out_specs=IN_VMEM,
        scratch_shapes=[pltpu.VMEM(rows.shape, jnp.float32)] * 2,
        compiler_params=pltpu.CompilerParams(vmem_limit_bytes=12 << 20),
        cost_estimate=pl.CostEstimate(flops=0, bytes_accessed=12 * rows.size, transcendentals=0),
        name="place_rows",
    )(index, rows)


def multiply_kernel(*refs):
    *part_refs, rows_ref, product_ref = refs
    blocks, own, _ = part_refs[0].shape
    total = jnp.zeros(product_ref.shape, jnp.float32)
    for i, part_ref in enumerate(part_refs):
        for block in range(blocks):
            rows = rows_ref[pl.ds((i * blocks + block) * own, own), :]
            total += jnp.dot(part_ref[block], rows, preferred_element_type=jnp.float32)
    product_ref[...] = total.astype(product_ref.dtype)


def multiply(parts, rows):
    own, columns = parts[0].shape[1], rows.shape[1]
    return pl.pallas_call(
        multiply_kernel,
        out_shape=jax.ShapeDtypeStruct((own, columns), rows.dtype),
        in_specs=[IN_VMEM] * (len(parts) + 1),
        out_specs=IN_VMEM,
        compiler_params=pltpu.CompilerParams(vmem_limit_bytes=8 << 20),
        cost_estimate=pl.CostEstimate(
            flops=2 * own * rows.size, bytes_accessed=4 * rows.size, transcendentals=0
        ),
        name="multiply_metric",
    )(*parts, rows)


BLOCKS_A_STEP = 4


def apply_kernel(_, *refs):
    *theta_refs, part_ref, total_ref, applied_ref, total = refs

    @pl.when(pl.program_id(0) == 0)
    def _():
        total[...] = total_ref[...]

    theta = jnp.concatenate([ref[...] for ref in theta_refs], axis=1)
    part = part_ref[pl.ds(pl.program_id(0) * BLOCKS_A_STEP, BLOCKS_A_STEP)]
    part = part.reshape(theta.shape[1], part_ref.shape[2])
    total[...] += jnp.dot(theta, part, preferred_element_type=jnp.float32)

    @pl.when(pl.program_id(0) == pl.num_programs(0) - 1)
    def _():
        applied_ref[...] = total[...].astype(applied_ref.dtype)


def apply(theta, part, first, total, dtype):
    rows = theta.shape[0]
    blocks, own, columns = part.shape
    if total is None:
        total = jnp.zeros((rows, columns), jnp.float32)

    def theta_spec(k):
        return pl.BlockSpec((rows, own), lambda i, first_ref: (0, first_ref[0] + (i * BLOCKS_A_STEP + k) * CORE))

    return pl.pallas_call(
        apply_kernel,
        out_shape=jax.ShapeDtypeStruct((rows, columns), dtype),
        grid_spec=pltpu.PrefetchScalarGridSpec(
            num_scalar_prefetch=1,
            grid=(blocks // BLOCKS_A_STEP,),
            in_specs=[
                *(theta_spec(k) for k in range(BLOCKS_A_STEP)),
                IN_VMEM,
                IN_VMEM,
            ],
            out_specs=IN_VMEM,
            scratch_shapes=[pltpu.VMEM((rows, columns), jnp.float32)],
        ),
        compiler_params=pltpu.CompilerParams(vmem_limit_bytes=50 << 20),
        cost_estimate=pl.CostEstimate(
            flops=2 * rows * part.size, bytes_accessed=2 * rows * blocks * own, transcendentals=0
        ),
        name="apply_theta",
    )(first.reshape(1), *([theta] * BLOCKS_A_STEP), part, total)


def take(rows, index):
    return jnp.take(rows, index, axis=0, mode="clip")


def shards(orbitals, points, theta, metric):
    row_count = orbitals.shape[0]
    point_count = points.shape[0]
    grid_count, band_count = lax.axis_size("grid"), lax.axis_size("band")
    me = lax.axis_index("grid")
    own = point_count // grid_count
    slots = jnp.arange(point_count, dtype=jnp.int32)
    by_owner, order = lax.sort_key_val(points, slots)
    my_rows = lax.dynamic_slice_in_dim(by_owner, me * own, own, 0) - me * row_count
    packed = take(orbitals, my_rows)
    along_z = gather_z(packed)
    metric_parts = gather_metric(metric.astype(jnp.bfloat16))
    gathered = gather_yc(along_z).reshape(point_count, -1)
    placing = lax.sort_key_val(order, slots)[1]
    placing = in_gather_order(placing // own) * own + placing % own

    my_points = take(gathered, lax.dynamic_slice_in_dim(placing, me * own, own, 0))
    partial_rows = lax.dot_general(
        gathered, my_points, (((1,), (1,)), ((), ())), preferred_element_type=jnp.float32
    ).astype(jnp.bfloat16)
    partial_rows = exchange_band(partial_rows.reshape(grid_count, own, own))
    blocks = [x + far + y for x in X_BITS for far in X_FAR for y in Y_HI]
    blocks = jnp.asarray(blocks, jnp.int32) ^ lax.axis_index("band")
    sampled = place(gathered, take(placing.reshape(band_count, own), blocks).reshape(point_count))
    product = multiply(metric_parts, sampled)
    products = gather_product(product).reshape(point_count, -1)
    density = jnp.sum(partial_rows.astype(jnp.float32), axis=0) * (1.0 / NB)
    squared = (density * density).astype(jnp.bfloat16)
    squared = exchange_band(spread(squared, band_count))
    order = order.reshape(Y, Z, CORE, own).swapaxes(1, 2).reshape(point_count)
    products = place(products, doubled_place(order // own ^ me, GRID_BITS) * own + order % own)
    coeffs = lax.dot_general(
        squared,
        products.reshape(grid_count, own, -1),
        (((0, 1), (0, 1)), ((), ())),
        preferred_element_type=jnp.float32,
    ).astype(jnp.bfloat16)
    coeffs = gather_z(coeffs)
    other_y = swap(coeffs, "grid", Z * CORE)
    other_core = swap(coeffs, "grid", 1)
    other_both = swap(other_y, "grid", 1)
    first = me // (Z * CORE) * (Z * CORE) + me % CORE
    total = None
    for name, part, bits in (
        ("own", coeffs, 0),
        ("core", other_core, 1),
        ("y", other_y, Z * CORE),
        ("both", other_both, Z * CORE + 1),
    ):
        dtype = jnp.bfloat16 if name == "both" else jnp.float32
        total = apply(theta, part, first ^ bits, total, dtype)
    return total


def solution(mesh):
    placed = (P("grid", "band"), P(), P("grid", None), P("grid", "band"))
    return jax.shard_map(shards, mesh=mesh, in_specs=placed, out_specs=P("grid", "band"), check_vma=False)
```
